32 devices in a mesh: groups: 2 (over y), chan: 4 (over z), tm: 2 (over x), sub: 2 (over core).
Axes of the slice: x: 2, y: 2, z: 4, core: 2. Of those that a mesh axis runs over, the one named last changes fastest.
Arguments:
- voltages: bfloat16 [2, 16, 1024, 8192], P(None, ('groups', 'tm'), None, ('chan', 'sub')), parts along dimension 1, may hold values from -200 to 200
- rfi_mask: int32 [16384], P(('groups', 'chan', 'sub')), parts along dimension 0, may hold values 0 or 1
- inner_delay: int32 [8192, 8], replicated, may hold values from 0 to 2
- pick: int32 [64, 128], replicated, may hold values from 0 to 7
- outer_delay: int32 [64, 128], replicated, may hold values from 0 to 2
Outputs:
- dedispersed: float32 [16, 1024, 128], P(('groups', 'tm'), ('chan', 'sub')), parts along dimension 0
The draws below stay inside these ranges and needn't reach their ends.
There are 2 independent parts, one for each index of `groups`. The reference program is written for one: setup_inputs(seed, part) draws one part's arguments, and reference() takes and returns one part's arrays. A program takes and returns all parts, laid end to end along the dimension named above; an argument that names none is the same for every part. Nothing has to cross between parts.
All inputs are finite; a program needn't handle non-finite values. No bound on the sum of `rfi_mask` on one device may be relied on, other than what follows from the above.
Results may differ from the reference program's by a relative error of at most 0.0013.
Values may be sent and summed in bfloat16 or wider, within the bound.
A program may use at most 128 MiB of HBM per device.

```python
import math
import jax
import jax.numpy as jnp
from jax import lax

NS = 256
EW = 4
FEEDS = 1024
BEAMS = 1024
CHANNELS = 8192
SUBW = 128
NSUB = 64
NJ = 8
NDM = 128
DIN = 2
DOUT = 2
TIME = 8


def draw_voltages(key, part):
    key_noise = jax.random.fold_in(key, 11)
    key_jitter = jax.random.fold_in(key, 12)
    key_gain = jax.random.fold_in(key, 13)
    time_frac = jnp.arange(TIME, dtype=jnp.float32) / max(TIME - 1, 1)
    rising = 1.0 + 2.0 * time_frac
    noise = jnp.clip(jax.random.normal(key_noise, (2, TIME, FEEDS, CHANNELS), jnp.float32), -4.0, 4.0)
    jitter = jnp.exp(jax.random.uniform(key_jitter, (TIME,), jnp.float32, -0.22, 0.22))
    chan_gain = jnp.exp(jax.random.uniform(key_gain, (CHANNELS,), jnp.float32, 0.0, math.log(10.0)))
    return (noise * (rising * jitter)[None, :, None, None] * chan_gain[None, None, None, :]).astype(jnp.bfloat16)


def set_ends(values, rng, smallest, top_value):
    longest = values.shape.index(max(values.shape))
    spots = []
    for shift in (0, 1):
        where = [jax.random.randint(jax.random.fold_in(rng, axis), (), 0, length) for axis, length in enumerate(values.shape)]
        where[longest] = (where[longest] + shift) % values.shape[longest]
        spots.append(tuple(where))
    return values.at[spots[0]].set(smallest).at[spots[1]].set(top_value)


def setup_inputs(seed: int = 0, part: int = 0) -> dict:
    keys = jax.random.split(jax.random.key(seed), 6)
    own_keys = jax.random.split(jax.random.fold_in(keys[5], part), 6)
    voltages = draw_voltages(jax.random.fold_in(jax.random.fold_in(keys[5], part), 71), part)
    rfi_mask = set_ends((jax.random.randint(own_keys[1], (CHANNELS,), 0, 8) < 7).astype(jnp.int32), jax.random.fold_in(own_keys[1], 1), 0, 1)
    inner_delay = set_ends(jax.random.randint(keys[2], (CHANNELS, NJ), 0, DIN + 1), jax.random.fold_in(keys[2], 1), 0, DIN).astype(jnp.int32)
    pick = set_ends(jax.random.randint(keys[3], (NSUB, NDM), 0, NJ), jax.random.fold_in(keys[3], 1), 0, NJ - 1).astype(jnp.int32)
    outer_delay = set_ends(jax.random.randint(keys[4], (NSUB, NDM), 0, DOUT + 1), jax.random.fold_in(keys[4], 1), 0, DOUT).astype(jnp.int32)
    return {"voltages": voltages, "rfi_mask": rfi_mask, "inner_delay": inner_delay, "pick": pick, "outer_delay": outer_delay}


eps_norm = 1e-05

def dft_tables(points):
    positions = jnp.arange(points, dtype=jnp.int32)
    products = positions[:, None] * positions[None, :] % points
    angle = products.astype(jnp.float32) * (2.0 * math.pi / points)
    return (jnp.cos(angle).astype(jnp.bfloat16), jnp.sin(angle).astype(jnp.bfloat16))

def east_west(real_part, imag_part):
    re0, re1, re2, re3 = (real_part[:, 0], real_part[:, 1], real_part[:, 2], real_part[:, 3])
    im0, im1, im2, im3 = (imag_part[:, 0], imag_part[:, 1], imag_part[:, 2], imag_part[:, 3])
    beam_real = jnp.stack([re0 + re1 + re2 + re3, re0 + im1 - re2 - im3, re0 - re1 + re2 - re3, re0 - im1 - re2 + im3], 1)
    beam_imag = jnp.stack([im0 + im1 + im2 + im3, im0 - re1 - im2 + re3, im0 - im1 + im2 - im3, im0 + re1 - im2 - re3], 1)
    return (beam_real, beam_imag)

def reference(voltages, rfi_mask, inner_delay, pick, outer_delay):
    dft_cos, dft_sin = dft_tables(NS)
    cos_full = dft_cos.astype(jnp.float32)
    sin_full = dft_sin.astype(jnp.float32)
    sample_count = TIME * BEAMS
    precise = lax.Precision.HIGHEST

    def one_subband(block_index):
        first_chan = (block_index * SUBW).astype(jnp.int32)
        volt_block = lax.dynamic_slice_in_dim(voltages, first_chan, SUBW, 3).astype(jnp.float32)
        volt_real = volt_block[0].reshape(TIME, EW, NS, SUBW)
        volt_imag = volt_block[1].reshape(TIME, EW, NS, SUBW)
        field_real = jnp.einsum('tenc,nm->temc', volt_real, cos_full, precision=precise) + jnp.einsum('tenc,nm->temc', volt_imag, sin_full, precision=precise)
        field_imag = jnp.einsum('tenc,nm->temc', volt_imag, cos_full, precision=precise) - jnp.einsum('tenc,nm->temc', volt_real, sin_full, precision=precise)
        beam_real, beam_imag = east_west(field_real, field_imag)
        intensity = (beam_real * beam_real + beam_imag * beam_imag).astype(jnp.bfloat16).reshape(TIME, BEAMS, SUBW)
        widened = intensity.astype(jnp.float32)
        chan_mean = lax.optimization_barrier(jnp.sum(widened, axis=(0, 1))) / sample_count
        centred = widened - chan_mean
        chan_var = lax.optimization_barrier(jnp.sum(centred * centred, axis=(0, 1))) / sample_count
        mask_block = lax.dynamic_slice_in_dim(rfi_mask, first_chan, SUBW, 0).astype(jnp.float32)
        normed = (centred * (lax.rsqrt(chan_var + eps_norm) * mask_block)).astype(jnp.bfloat16)
        delays = lax.dynamic_slice_in_dim(inner_delay, first_chan, SUBW, 0)
        padded = jnp.concatenate([jnp.zeros((DIN, BEAMS, SUBW), jnp.bfloat16), normed], 0)
        totals = jnp.zeros((TIME, BEAMS, NJ), jnp.float32)
        for delay_value in range(DIN + 1):
            selector = (delays == delay_value).astype(jnp.float32)
            window = padded[DIN - delay_value:DIN - delay_value + TIME].astype(jnp.float32)
            totals = totals + jnp.einsum('tbw,wj->tbj', window, selector, precision=precise)
        return (totals * (1.0 / math.sqrt(SUBW))).astype(jnp.bfloat16)
    stacked = lax.map(one_subband, jnp.arange(NSUB, dtype=jnp.int32))
    partial_value = jnp.transpose(stacked, (1, 2, 0, 3)).reshape(TIME, BEAMS, NSUB * NJ)
    padded = jnp.concatenate([jnp.zeros((DOUT, BEAMS, NSUB * NJ), jnp.bfloat16), partial_value], 0).astype(jnp.float32)
    slot_ids = jnp.arange(NJ, dtype=jnp.int32)
    totals = jnp.zeros((TIME, BEAMS, NDM), jnp.float32)
    for delay_value in range(DOUT + 1):
        chosen = (pick[:, None, :] == slot_ids[None, :, None]) & (outer_delay[:, None, :] == delay_value)
        selector = chosen.astype(jnp.float32).reshape(NSUB * NJ, NDM)
        window = padded[DOUT - delay_value:DOUT - delay_value + TIME]
        totals = totals + jnp.einsum('tbw,wk->tbk', window, selector, precision=precise)
    return totals * (1.0 / math.sqrt(NSUB))
```

```python
import functools
import math

import jax
import jax.numpy as jnp
import numpy as np
from jax import lax
from jax.experimental import pallas as pl
from jax.experimental.pallas import tpu as pltpu
from jax.sharding import PartitionSpec as P

NS = 256
EW = 4
BEAMS = 1024
SUBW = 128
DIN = 2
DOUT = 2
NJ = 8
LANES = 128

eps_norm = 1e-05
MESH = pl.DeviceIdType.MESH


def dft_matrix(points):
    positions = np.arange(points, dtype=np.int32)
    products = positions[:, None] * positions[None, :] % points
    angle = products.astype(np.float32) * np.float32(2.0 * math.pi / points)
    cos, sin = np.cos(angle), np.sin(angle)
    table = np.concatenate(
        [np.concatenate([cos.T, sin.T], 1), np.concatenate([-sin.T, cos.T], 1)], 0
    )
    return table.astype(jnp.bfloat16)


def kernel(
    cfg,
    volt_hbm,
    table_ref,
    mask_ref,
    delay_hbm,
    pick_ref,
    outer_ref,
    out_ref,
    vbuf,
    inten,
    field0,
    field1,
    delay_v,
    sel1,
    sel2,
    pilot,
    acc1,
    acc2,
    stats,
    part_acc,
    carry_out,
    carry_in,
    send_buf,
    recv_buf,
    carry2_out,
    carry2_in,
    vsem,
    dsem,
    stat_send,
    stat_recv,
    carry_send,
    carry_recv,
    turn_send,
    turn_recv,
    own_sem,
    carry2_send,
    carry2_recv,
):
    rows, chans, ct, ntm, nsub, ndev, ndm = (
        cfg["rows"], cfg["chans"], cfg["ct"], cfg["ntm"], cfg["nsub"], cfg["ndev"], cfg["ndm"],
    )
    pairs = rows // 2
    ctiles = chans // ct
    steps = rows * ctiles
    local_beams = BEAMS // ndev
    subs = chans // SUBW
    width = subs * NJ
    rb_rows = cfg["rb"]
    nrb = BEAMS // rb_rows
    tm = lax.axis_index("tm")
    me = lax.axis_index("chan") * nsub + lax.axis_index("sub")

    def peer_id(index):
        return {"chan": index // nsub, "sub": lax.rem(index, nsub)}

    def volt_copy(step):
        t, tile = step // ctiles, lax.rem(step, ctiles)
        return pltpu.make_async_copy(
            volt_hbm.at[:, t, :, pl.ds(pl.multiple_of(tile * ct, ct), ct)],
            vbuf.at[step],
            vsem.at[step],
        )

    def start_volt(step, carry):
        volt_copy(step).start()
        return carry

    lax.fori_loop(0, steps, start_volt, 0)
    delay_copy = pltpu.make_async_copy(
        delay_hbm.at[:, pl.ds(pl.multiple_of(me * chans, chans), chans)], delay_v, dsem
    )
    delay_copy.start()

    barrier = pltpu.get_barrier_semaphore()

    def greet_tm(k, carry):
        pl.semaphore_signal(
            barrier, inc=1, device_id={"tm": lax.rem(tm + k, ntm)}, device_id_type=MESH
        )
        return carry

    def greet_turn(k, carry):
        pl.semaphore_signal(
            barrier, inc=1, device_id=peer_id(lax.rem(me + k, ndev)), device_id_type=MESH
        )
        return carry

    lax.fori_loop(1, ntm, greet_tm, 0)
    lax.fori_loop(1, ndev, greet_turn, 0)

    delay_copy.wait()
    delays = delay_v[...].astype(jnp.float32)
    chan_sub = lax.broadcasted_iota(jnp.int32, (NJ, chans), 1) // SUBW
    for par_in in range(2):
        for half in range(2):
            pieces = []
            for group in range(LANES // NJ):
                par_out, sub = group // subs, group % subs
                lag = 2 * half + par_out - par_in
                if group < 2 * subs and 0 <= lag <= DIN:
                    hit = (delays == float(lag)) & (chan_sub == sub)
                    pieces.append(jnp.where(hit, 1.0, 0.0))
                else:
                    pieces.append(jnp.zeros((NJ, chans), jnp.float32))
            sel1[par_in, half * LANES : (half + 1) * LANES, :] = jnp.concatenate(
                pieces, 0
            ).astype(jnp.bfloat16)
    nsubs_all = subs * ndev
    code = (pick_ref[...] + NJ * outer_ref[...]).astype(jnp.float32).astype(jnp.bfloat16)

    def make_sel2(dev, carry):
        q = lax.broadcasted_iota(jnp.int32, (LANES, nsubs_all), 0)
        which = dev * subs + lax.rem(q, width) // NJ
        expand = jnp.where(
            which == lax.broadcasted_iota(jnp.int32, (LANES, nsubs_all), 1), 1.0, 0.0
        ).astype(jnp.bfloat16)
        spread = jnp.dot(expand, code, preferred_element_type=jnp.float32)
        q = lax.broadcasted_iota(jnp.int32, (LANES, ndm), 0)
        slot = lax.rem(q, NJ)
        par_in = q // width
        base = pl.multiple_of(dev * LANES, LANES)
        for half in range(2):
            for par_out in range(2):
                lag = 2 * half + par_out - par_in
                want = (slot + NJ * lag).astype(jnp.float32)
                hit = (spread == want) & (lag >= 0) & (lag <= DOUT) & (par_in < 2)
                col = (2 * half + par_out) * ndm
                sel2[pl.ds(base, LANES), col : col + ndm] = jnp.where(hit, 1.0, 0.0).astype(
                    jnp.bfloat16
                )
        return carry

    lax.fori_loop(0, ndev, make_sel2, 0)
    pilot[...] = jnp.zeros_like(pilot)
    acc1[...] = jnp.zeros_like(acc1)
    acc2[...] = jnp.zeros_like(acc2)

    @pl.when(tm == 0)
    def _():
        carry_in[...] = jnp.zeros_like(carry_in)
        carry2_in[...] = jnp.zeros_like(carry2_in)

    def transform(step, field):
        volt_copy(step).wait()
        for e in range(EW):
            block = vbuf[step, :, e * NS : (e + 1) * NS, :].reshape(2 * NS, ct)
            field[e] = jnp.dot(table_ref[...], block, preferred_element_type=jnp.float32)

    CH = 16

    def fold8(x):
        return x[:8] + x[8:]

    def detect(step, field):
        t, tile = step // ctiles, lax.rem(step, ctiles)
        shift = jnp.broadcast_to(pilot[tile], (CH, ct))
        s1 = jnp.zeros((8, ct), jnp.float32)
        s2 = jnp.zeros((8, ct), jnp.float32)
        col = pl.ds(pl.multiple_of(tile * ct, ct), ct)
        for chunk in range(NS // CH):
            lo = chunk * CH
            re = [field[e, lo : lo + CH, :] for e in range(EW)]
            im = [field[e, NS + lo : NS + lo + CH, :] for e in range(EW)]
            ra, rb, rc, rd = re[0] + re[2], re[0] - re[2], re[1] + re[3], re[1] - re[3]
            ia, ib, ic, id_ = im[0] + im[2], im[0] - im[2], im[1] + im[3], im[1] - im[3]
            beam = [
                (ra + rc, ia + ic),
                (rb + id_, ib - rd),
                (ra - rc, ia - ic),
                (rb - id_, ib + rd),
            ]
            for q in range(EW):
                x = beam[q][0] * beam[q][0] + beam[q][1] * beam[q][1]
                x = x.astype(jnp.bfloat16)
                inten[t, q * NS + lo : q * NS + lo + CH, col] = x
                dev = x.astype(jnp.float32) - shift
                s1 = s1 + fold8(dev)
                s2 = s2 + fold8(dev * dev)

        @pl.when(t > 0)
        def _():
            acc1[tile] += s1
            acc2[tile] += s2

        @pl.when(t == 0)
        def _():
            mean = jnp.sum(s1, axis=0, keepdims=True) * (1.0 / BEAMS)
            pilot[tile] = mean
            wide = jnp.broadcast_to(mean, (CH, ct))

            def again(chunk, sums):
                r1, r2 = sums
                lo = pl.multiple_of(chunk * 4 * CH, 4 * CH)
                for i in range(4):
                    x = inten[0, pl.ds(lo + i * CH, CH), col].astype(jnp.float32)
                    dev = x - wide
                    r1 = r1 + fold8(dev)
                    r2 = r2 + fold8(dev * dev)
                return r1, r2

            zero = jnp.zeros((8, ct), jnp.float32)
            r1, r2 = lax.fori_loop(0, BEAMS // (4 * CH), again, (zero, zero))
            acc1[tile] = r1
            acc2[tile] = r2

    transform(0, field0)

    def two_steps(i, carry):
        transform(2 * i + 1, field1)
        detect(2 * i, field0)

        @pl.when(2 * i + 2 < steps)
        def _():
            transform(2 * i + 2, field0)

        detect(2 * i + 1, field1)
        return carry

    lax.fori_loop(0, steps // 2, two_steps, 0)

    count = float(rows * BEAMS)
    for tile in range(ctiles):
        s1 = jnp.sum(acc1[tile], axis=0, keepdims=True)
        s2 = jnp.sum(acc2[tile], axis=0, keepdims=True)
        cols = slice(tile * ct, (tile + 1) * ct)
        stats[tm, 0:1, cols] = pilot[tile] + s1 * (1.0 / count)
        stats[tm, 1:2, cols] = s2 - s1 * s1 * (1.0 / count)

    pl.semaphore_wait(barrier, ntm - 1 + ndev - 1)

    def stat_copy(k, sender):
        return pltpu.make_async_remote_copy(
            src_ref=stats.at[tm],
            dst_ref=stats.at[sender],
            send_sem=stat_send.at[k],
            recv_sem=stat_recv.at[k],
            device_id={"tm": lax.rem(tm + k, ntm)},
            device_id_type=MESH,
        )

    for k in range(1, ntm):
        stat_copy(k, tm).start()
    for k in range(1, ntm):
        stat_copy(k, lax.rem(tm + ntm - k, ntm)).wait_recv()
    means = [stats[i, 0:1, :] for i in range(ntm)]
    mean = sum(means[1:], means[0]) * (1.0 / ntm)
    spread = sum(stats[i, 1:2, :] for i in range(ntm))
    for i in range(ntm):
        spread = spread + count * ((means[i] - mean) * (means[i] - mean))
    var = spread * (1.0 / (count * ntm))
    scale = lax.rsqrt(var + eps_norm) * mask_ref[...].astype(jnp.float32)

    def carry_copy(rb):
        return pltpu.make_async_remote_copy(
            src_ref=carry_out.at[rb],
            dst_ref=carry_in.at[rb],
            send_sem=carry_send.at[rb],
            recv_sem=carry_recv.at[rb],
            device_id={"tm": lax.rem(tm + 1, ntm)},
            device_id_type=MESH,
        )

    def level1(pair, rb):
        lo = pl.multiple_of(rb * rb_rows, rb_rows)
        total = None
        for par in range(2):
            x = inten[2 * pair + par, pl.ds(lo, rb_rows), :].astype(jnp.float32)
            normed = ((x - mean) * scale).astype(jnp.bfloat16)
            term = lax.dot_general(
                normed, sel1[par], (((1,), (1,)), ((), ())), preferred_element_type=jnp.float32
            )
            total = term if total is None else total + term
        return lo, total

    inv1 = 1.0 / math.sqrt(SUBW)

    def put_send(pair, lo, total):
        send_buf[pair, pl.ds(lo, rb_rows), :] = (total * inv1).astype(jnp.bfloat16)

    def turn_copy(pair, k, sender):
        peer = lax.rem(me + k, ndev)
        return pltpu.make_async_remote_copy(
            src_ref=send_buf.at[
                pair, pl.ds(pl.multiple_of(peer * local_beams, local_beams), local_beams), :
            ],
            dst_ref=recv_buf.at[pair, :, pl.ds(pl.multiple_of(sender * LANES, LANES), LANES)],
            send_sem=turn_send.at[pair, k],
            recv_sem=turn_recv.at[pair, k],
            device_id=peer_id(peer),
            device_id_type=MESH,
        )

    def own_copy(pair):
        return pltpu.make_async_copy(
            send_buf.at[
                pair, pl.ds(pl.multiple_of(me * local_beams, local_beams), local_beams), :
            ],
            recv_buf.at[pair, :, pl.ds(pl.multiple_of(me * LANES, LANES), LANES)],
            own_sem.at[pair],
        )

    def start_turn(pair):
        def one(k, carry):
            turn_copy(pair, k, me).start()
            return carry

        lax.fori_loop(1, ndev, one, 0)
        own_copy(pair).start()

    last = pairs - 1
    for pair in range(last, -1, -1):

        def block(rb, carry, pair=pair):
            lo, total = level1(pair, rb)
            if pair == last:
                carry_out[rb] = total[:, LANES:]

                @pl.when(tm < ntm - 1)
                def _():
                    carry_copy(rb).start()

            else:
                put_send(pair + 1, lo, part_acc[pair + 1, pl.ds(lo, rb_rows), :] + total[:, LANES:])
            part_acc[pair, pl.ds(lo, rb_rows), :] = total[:, :LANES]
            return carry

        lax.fori_loop(0, nrb, block, 0)
        if pair < last:
            start_turn(pair + 1)

    def finish(rb, carry):
        @pl.when(tm > 0)
        def _():
            carry_copy(rb).wait_recv()

        lo = pl.multiple_of(rb * rb_rows, rb_rows)
        put_send(0, lo, part_acc[0, pl.ds(lo, rb_rows), :] + carry_in[rb])
        return carry

    lax.fori_loop(0, nrb, finish, 0)
    start_turn(0)

    carry2_copy = pltpu.make_async_remote_copy(
        src_ref=carry2_out,
        dst_ref=carry2_in,
        send_sem=carry2_send,
        recv_sem=carry2_recv,
        device_id={"tm": lax.rem(tm + 1, ntm)},
        device_id_type=MESH,
    )
    inv2 = 1.0 / math.sqrt(nsubs_all)
    held = None
    for pair in range(last, -1, -1):

        def arrive(k, carry, pair=pair):
            turn_copy(pair, k, lax.rem(me + ndev - k, ndev)).wait_recv()
            return carry

        lax.fori_loop(1, ndev, arrive, 0)
        own_copy(pair).wait()
        merged = jnp.dot(recv_buf[pair], sel2[...], preferred_element_type=jnp.float32)
        if pair == last:
            carry2_out[...] = merged[:, 2 * ndm :]

            @pl.when(tm < ntm - 1)
            def _():
                carry2_copy.start()

        else:
            held = held + merged[:, 2 * ndm :]
            out_ref[2 * pair + 2] = held[:, :ndm] * inv2
            out_ref[2 * pair + 3] = held[:, ndm:] * inv2
        held = merged[:, : 2 * ndm]

    @pl.when(tm > 0)
    def _():
        carry2_copy.wait_recv()

    held = held + carry2_in[...]
    out_ref[0] = held[:, :ndm] * inv2
    out_ref[1] = held[:, ndm:] * inv2

    for k in range(1, ntm):
        stat_copy(k, tm).wait_send()

    @pl.when(tm < ntm - 1)
    def _():
        def sent(rb, carry):
            carry_copy(rb).wait_send()
            return carry

        lax.fori_loop(0, nrb, sent, 0)
        carry2_copy.wait_send()

    for pair in range(pairs):

        def left(k, carry, pair=pair):
            turn_copy(pair, k, me).wait_send()
            return carry

        lax.fori_loop(1, ndev, left, 0)


def body(voltages, rfi_mask, inner_delay, pick, outer_delay):
    rows, chans = voltages.shape[1], voltages.shape[3]
    ntm, nsub = lax.axis_size("tm"), lax.axis_size("sub")
    ndev = lax.axis_size("chan") * nsub
    ndm = pick.shape[1]
    ct = min(256, chans)
    ctiles = chans // ct
    pairs = rows // 2
    rb = 256
    nrb = BEAMS // rb
    lb = BEAMS // ndev
    cfg = dict(rows=rows, chans=chans, ct=ct, ntm=ntm, nsub=nsub, ndev=ndev, ndm=ndm, rb=rb)
    f32, bf16 = jnp.float32, jnp.bfloat16
    vm = pl.BlockSpec(memory_space=pltpu.VMEM)
    hbm = pl.BlockSpec(memory_space=pl.ANY)
    dma, steps = pltpu.SemaphoreType.DMA, rows * ctiles
    return pl.pallas_call(
        functools.partial(kernel, cfg),
        out_shape=jax.ShapeDtypeStruct((rows, lb, ndm), f32),
        in_specs=[hbm, vm, vm, hbm, vm, vm],
        out_specs=vm,
        scratch_shapes=[
            pltpu.VMEM((steps, 2, EW * NS, ct), bf16),
            pltpu.VMEM((rows, BEAMS, chans), bf16),
            pltpu.VMEM((EW, 2 * NS, ct), f32),
            pltpu.VMEM((EW, 2 * NS, ct), f32),
            pltpu.VMEM((NJ, chans), jnp.int32),
            pltpu.VMEM((2, 2 * LANES, chans), bf16),
            pltpu.VMEM((ndev * LANES, 4 * ndm), bf16),
            pltpu.VMEM((ctiles, 1, ct), f32),
            pltpu.VMEM((ctiles, 8, ct), f32),
            pltpu.VMEM((ctiles, 8, ct), f32),
            pltpu.VMEM((ntm, 2, chans), f32),
            pltpu.VMEM((pairs, BEAMS, LANES), f32),
            pltpu.VMEM((nrb, rb, LANES), f32),
            pltpu.VMEM((nrb, rb, LANES), f32),
            pltpu.VMEM((pairs, BEAMS, LANES), bf16),
            pltpu.VMEM((pairs, lb, ndev * LANES), bf16),
            pltpu.VMEM((lb, 2 * ndm), f32),
            pltpu.VMEM((lb, 2 * ndm), f32),
            dma((steps,)),
            dma,
            dma((ntm,)),
            dma((ntm,)),
            dma((nrb,)),
            dma((nrb,)),
            dma((pairs, ndev)),
            dma((pairs, ndev)),
            dma((pairs,)),
            dma,
            dma,
        ],
        compiler_params=pltpu.CompilerParams(
            collective_id=0, has_side_effects=True, vmem_limit_bytes=60 * 2**20
        ),
    )(
        voltages,
        jnp.asarray(dft_matrix(NS)),
        rfi_mask.reshape(1, chans),
        inner_delay.T,
        pick,
        outer_delay,
    )


def solution(mesh):
    placed = (
        P(None, ("groups", "tm"), None, ("chan", "sub")),
        P(("groups", "chan", "sub")),
        P(),
        P(),
        P(),
    )
    return jax.shard_map(
        body,
        mesh=mesh,
        in_specs=placed,
        out_specs=P(("groups", "tm"), ("chan", "sub"), None),
        check_vma=False,
    )
```

```python
import functools
import math

import jax
import jax.numpy as jnp
import numpy as np
from jax import lax
from jax.experimental import pallas as pl
from jax.experimental.pallas import tpu as pltpu
from jax.sharding import PartitionSpec as P

NS = 256
EW = 4
BEAMS = 1024
SUBW = 128
DIN = 2
DOUT = 2
NJ = 8
LANES = 128

eps_norm = 1e-05
MESH = pl.DeviceIdType.MESH


def dft_matrix(points):
    positions = np.arange(points, dtype=np.int32)
    products = positions[:, None] * positions[None, :] % points
    angle = products.astype(np.float32) * np.float32(2.0 * math.pi / points)
    half = points // 2
    cos, sin = np.cos(angle), np.sin(angle)
    table = np.concatenate([cos[:half], cos[half : half + 1], sin[1:half]], 0)
    return table.astype(jnp.bfloat16)


def kernel(
    cfg,
    volt_hbm,
    table_ref,
    mask_ref,
    delay_hbm,
    pick_ref,
    outer_ref,
    out_ref,
    vbuf,
    inten,
    field0,
    field1,
    delay_v,
    sel1,
    sel2,
    pilot,
    acc1,
    acc2,
    stats,
    part_acc,
    carry_out,
    carry_in,
    send_buf,
    recv_buf,
    carry2_out,
    carry2_in,
    vsem,
    dsem,
    stat_send,
    stat_recv,
    carry_send,
    carry_recv,
    turn_send,
    turn_recv,
    own_sem,
    carry2_send,
    carry2_recv,
):
    rows, chans, ct, ntm, nsub, ndev, ndm = (
        cfg["rows"], cfg["chans"], cfg["ct"], cfg["ntm"], cfg["nsub"], cfg["ndev"], cfg["ndm"],
    )
    pairs = rows // 2
    ctiles = chans // ct
    steps = rows * ctiles
    local_beams = BEAMS // ndev
    subs = chans // SUBW
    width = subs * NJ
    rb_rows = cfg["rb"]
    nrb = BEAMS // rb_rows
    tm = lax.axis_index("tm")
    me = lax.axis_index("chan") * nsub + lax.axis_index("sub")

    def peer_id(index):
        return {"chan": index // nsub, "sub": lax.rem(index, nsub)}

    def volt_copy(step):
        t, tile = step // ctiles, lax.rem(step, ctiles)
        return pltpu.make_async_copy(
            volt_hbm.at[:, t, :, pl.ds(pl.multiple_of(tile * ct, ct), ct)],
            vbuf.at[step],
            vsem.at[step],
        )

    def start_volt(step, carry):
        volt_copy(step).start()
        return carry

    lax.fori_loop(0, steps, start_volt, 0)
    delay_copy = pltpu.make_async_copy(
        delay_hbm.at[:, pl.ds(pl.multiple_of(me * chans, chans), chans)], delay_v, dsem
    )
    delay_copy.start()

    barrier = pltpu.get_barrier_semaphore()

    def greet_tm(k, carry):
        pl.semaphore_signal(
            barrier, inc=1, device_id={"tm": lax.rem(tm + k, ntm)}, device_id_type=MESH
        )
        return carry

    def greet_turn(k, carry):
        pl.semaphore_signal(
            barrier, inc=1, device_id=peer_id(lax.rem(me + k, ndev)), device_id_type=MESH
        )
        return carry

    lax.fori_loop(1, ntm, greet_tm, 0)
    lax.fori_loop(1, ndev, greet_turn, 0)

    pilot[...] = jnp.zeros_like(pilot)
    acc1[...] = jnp.zeros_like(acc1)
    acc2[...] = jnp.zeros_like(acc2)

    @pl.when(tm == 0)
    def _():
        carry_in[...] = jnp.zeros_like(carry_in)
        carry2_in[...] = jnp.zeros_like(carry2_in)

    def transform(step, field):
        volt_copy(step).wait()
        for e in range(EW):
            for part in range(2):
                block = vbuf[step, part, e * NS : (e + 1) * NS, :]
                field[e, part * NS : (part + 1) * NS, :] = jnp.dot(
                    table_ref[...], block, preferred_element_type=jnp.float32
                )

    CH, HALF = 16, NS // 2

    def fold8(x):
        return x[:8] + x[8:]

    def detect(step, field):
        t, tile = step // ctiles, lax.rem(step, ctiles)
        col = pl.ds(pl.multiple_of(tile * ct, ct), ct)
        wide_row = pilot[tile]
        sums1, sums2 = [], []
        top = lax.broadcasted_iota(jnp.int32, (CH, LANES), 0) == 0
        for lane in range(0, ct, LANES):
            shift = jnp.broadcast_to(wide_row[:, lane : lane + LANES], (CH, LANES))
            s1 = jnp.zeros((8, LANES), jnp.float32)
            s2 = jnp.zeros((8, LANES), jnp.float32)
            here = pl.ds(pl.multiple_of(tile * ct + lane, LANES), LANES)
            for chunk in range(HALF // CH):
                lo = chunk * CH

                def part(index):
                    at = index * HALF + lo
                    return [field[e, at : at + CH, lane : lane + LANES] for e in range(EW)]

                ca, sb, cb, sa = part(0), part(1), part(2), part(3)
                if chunk == 0:
                    sa0 = [jnp.where(top, 0.0, v) for v in sa]
                    sb0 = [jnp.where(top, 0.0, v) for v in sb]
                else:
                    sa0, sb0 = sa, sb
                for mirror in range(2):
                    if mirror == 0:
                        re = [u + v for u, v in zip(ca, sa0)]
                        im = [u - v for u, v in zip(cb, sb0)]
                    else:
                        re = [u - v for u, v in zip(ca, sa0)]
                        im = [u + v for u, v in zip(cb, sb0)]
                        if chunk == 0:
                            re = [jnp.where(top, v, u) for u, v in zip(re, sb)]
                            im = [jnp.where(top, v, u) for u, v in zip(im, sa)]
                    ra, rb, rc, rd = re[0] + re[2], re[0] - re[2], re[1] + re[3], re[1] - re[3]
                    ia, ib, ic, id_ = im[0] + im[2], im[0] - im[2], im[1] + im[3], im[1] - im[3]
                    beam = [
                        (ra + rc, ia + ic),
                        (rb + id_, ib - rd),
                        (ra - rc, ia - ic),
                        (rb - id_, ib + rd),
                    ]
                    for q in range(EW):
                        x = beam[q][0] * beam[q][0] + beam[q][1] * beam[q][1]
                        x = x.astype(jnp.bfloat16)
                        at = q * NS + mirror * HALF + lo
                        inten[t, at : at + CH, here] = x
                        dev = x.astype(jnp.float32) - shift
                        s1 = s1 + fold8(dev)
                        s2 = s2 + fold8(dev * dev)
            sums1.append(s1)
            sums2.append(s2)
        s1, s2 = jnp.concatenate(sums1, 1), jnp.concatenate(sums2, 1)

        @pl.when(t > 0)
        def _():
            acc1[tile] += s1
            acc2[tile] += s2

        @pl.when(t == 0)
        def _():
            mean = jnp.sum(s1, axis=0, keepdims=True) * (1.0 / BEAMS)
            pilot[tile] = mean
            wide = jnp.broadcast_to(mean, (CH, ct))

            def again(chunk, sums):
                r1, r2 = sums
                lo = pl.multiple_of(chunk * 4 * CH, 4 * CH)
                for i in range(4):
                    x = inten[0, pl.ds(lo + i * CH, CH), col].astype(jnp.float32)
                    dev = x - wide
                    r1 = r1 + fold8(dev)
                    r2 = r2 + fold8(dev * dev)
                return r1, r2

            zero = jnp.zeros((8, ct), jnp.float32)
            r1, r2 = lax.fori_loop(0, BEAMS // (4 * CH), again, (zero, zero))
            acc1[tile] = r1
            acc2[tile] = r2

    transform(0, field0)

    def two_steps(i, carry):
        transform(2 * i + 1, field1)
        detect(2 * i, field0)

        transform(2 * i + 2, field0)
        detect(2 * i + 1, field1)
        return carry

    lax.fori_loop(0, steps // 2 - 1, two_steps, 0)
    transform(steps - 1, field1)
    detect(steps - 2, field0)
    detect(steps - 1, field1)

    count = float(rows * BEAMS)
    for tile in range(ctiles):
        s1 = jnp.sum(acc1[tile], axis=0, keepdims=True)
        s2 = jnp.sum(acc2[tile], axis=0, keepdims=True)
        cols = slice(tile * ct, (tile + 1) * ct)
        stats[tm, 0:1, cols] = pilot[tile] + s1 * (1.0 / count)
        stats[tm, 1:2, cols] = s2 - s1 * s1 * (1.0 / count)

    pl.semaphore_wait(barrier, ntm - 1 + ndev - 1)

    def stat_copy(k, sender):
        return pltpu.make_async_remote_copy(
            src_ref=stats.at[tm],
            dst_ref=stats.at[sender],
            send_sem=stat_send.at[k],
            recv_sem=stat_recv.at[k],
            device_id={"tm": lax.rem(tm + k, ntm)},
            device_id_type=MESH,
        )

    for k in range(1, ntm):
        stat_copy(k, tm).start()
    delay_copy.wait()
    delays = delay_v[...].astype(jnp.float32)
    chan_sub = lax.broadcasted_iota(jnp.int32, (NJ, chans), 1) // SUBW
    for par_in in range(2):
        for half in range(2):
            pieces = []
            for group in range(LANES // NJ):
                par_out, sub = group // subs, group % subs
                lag = 2 * half + par_out - par_in
                if group < 2 * subs and 0 <= lag <= DIN:
                    hit = (delays == float(lag)) & (chan_sub == sub)
                    pieces.append(jnp.where(hit, 1.0, 0.0))
                else:
                    pieces.append(jnp.zeros((NJ, chans), jnp.float32))
            sel1[par_in, half * LANES : (half + 1) * LANES, :] = jnp.concatenate(
                pieces, 0
            ).astype(jnp.bfloat16)
    for k in range(1, ntm):
        stat_copy(k, lax.rem(tm + ntm - k, ntm)).wait_recv()
    means = [stats[i, 0:1, :] for i in range(ntm)]
    mean = sum(means[1:], means[0]) * (1.0 / ntm)
    spread = sum(stats[i, 1:2, :] for i in range(ntm))
    for i in range(ntm):
        spread = spread + count * ((means[i] - mean) * (means[i] - mean))
    var = spread * (1.0 / (count * ntm))
    scale = lax.rsqrt(var + eps_norm) * mask_ref[...].astype(jnp.float32)

    def carry_copy(rb):
        return pltpu.make_async_remote_copy(
            src_ref=carry_out.at[rb],
            dst_ref=carry_in.at[rb],
            send_sem=carry_send.at[rb],
            recv_sem=carry_recv.at[rb],
            device_id={"tm": lax.rem(tm + 1, ntm)},
            device_id_type=MESH,
        )

    def level1(pair, rb):
        lo = pl.multiple_of(rb * rb_rows, rb_rows)
        total = None
        for par in range(2):
            x = inten[2 * pair + par, pl.ds(lo, rb_rows), :].astype(jnp.float32)
            normed = ((x - mean) * scale).astype(jnp.bfloat16)
            term = lax.dot_general(
                normed, sel1[par], (((1,), (1,)), ((), ())), preferred_element_type=jnp.float32
            )
            total = term if total is None else total + term
        return lo, total

    inv1 = 1.0 / math.sqrt(SUBW)
    to_row = lax.broadcasted_iota(jnp.int32, (HALF, HALF), 0)
    from_row = lax.broadcasted_iota(jnp.int32, (HALF, HALF), 1)
    flip = jnp.where(lax.rem(to_row + from_row, HALF) == 0, 1.0, 0.0).astype(jnp.bfloat16)

    def put_send(pair, lo, total):
        ready = (total * inv1).astype(jnp.bfloat16)
        send_buf[pair, pl.ds(lo, HALF), :] = ready[:HALF]
        send_buf[pair, pl.ds(lo + HALF, HALF), :] = jnp.dot(
            flip, ready[HALF:], preferred_element_type=jnp.float32
        ).astype(jnp.bfloat16)

    def turn_copy(pair, k, sender):
        peer = lax.rem(me + k, ndev)
        return pltpu.make_async_remote_copy(
            src_ref=send_buf.at[
                pair, pl.ds(pl.multiple_of(peer * local_beams, local_beams), local_beams), :
            ],
            dst_ref=recv_buf.at[pair, :, pl.ds(pl.multiple_of(sender * LANES, LANES), LANES)],
            send_sem=turn_send.at[pair, k],
            recv_sem=turn_recv.at[pair, k],
            device_id=peer_id(peer),
            device_id_type=MESH,
        )

    def own_copy(pair):
        return pltpu.make_async_copy(
            send_buf.at[
                pair, pl.ds(pl.multiple_of(me * local_beams, local_beams), local_beams), :
            ],
            recv_buf.at[pair, :, pl.ds(pl.multiple_of(me * LANES, LANES), LANES)],
            own_sem.at[pair],
        )

    peers_rb = max(1, ndev // nrb)
    first_rb = me // peers_rb

    def start_turn(pair, rb):
        def one(i, carry):
            k = lax.rem(rb * peers_rb + i + ndev - me, ndev)

            @pl.when(k > 0)
            def _():
                turn_copy(pair, k, me).start()

            @pl.when(k == 0)
            def _():
                own_copy(pair).start()

            return carry

        lax.fori_loop(0, peers_rb, one, 0)

    last = pairs - 1
    for pair in range(last, -1, -1):

        def block(i, carry, pair=pair):
            rb = lax.rem(first_rb + i, nrb)
            lo, total = level1(pair, rb)
            if pair == last:
                carry_out[rb] = total[:, LANES:]

                @pl.when(tm < ntm - 1)
                def _():
                    carry_copy(rb).start()

            else:
                put_send(pair + 1, lo, part_acc[pair + 1, pl.ds(lo, rb_rows), :] + total[:, LANES:])
                start_turn(pair + 1, rb)
            part_acc[pair, pl.ds(lo, rb_rows), :] = total[:, :LANES]
            return carry

        lax.fori_loop(0, nrb, block, 0)

    nsubs_all = subs * ndev
    code = (pick_ref[...] + NJ * outer_ref[...]).astype(jnp.float32).astype(jnp.bfloat16)

    def make_sel2(dev, carry):
        q = lax.broadcasted_iota(jnp.int32, (LANES, nsubs_all), 0)
        which = dev * subs + lax.rem(q, width) // NJ
        expand = jnp.where(
            which == lax.broadcasted_iota(jnp.int32, (LANES, nsubs_all), 1), 1.0, 0.0
        ).astype(jnp.bfloat16)
        spread = jnp.dot(expand, code, preferred_element_type=jnp.float32)
        q = lax.broadcasted_iota(jnp.int32, (LANES, ndm), 0)
        slot = lax.rem(q, NJ)
        par_in = q // width
        base = pl.multiple_of(dev * LANES, LANES)
        for half in range(2):
            for par_out in range(2):
                lag = 2 * half + par_out - par_in
                want = (slot + NJ * lag).astype(jnp.float32)
                hit = (spread == want) & (lag >= 0) & (lag <= DOUT) & (par_in < 2)
                col = (2 * half + par_out) * ndm
                sel2[pl.ds(base, LANES), col : col + ndm] = jnp.where(hit, 1.0, 0.0).astype(
                    jnp.bfloat16
                )
        return carry

    lax.fori_loop(0, ndev, make_sel2, 0)

    def finish(i, carry):
        rb = lax.rem(first_rb + i, nrb)

        @pl.when(tm > 0)
        def _():
            carry_copy(rb).wait_recv()

        lo = pl.multiple_of(rb * rb_rows, rb_rows)
        put_send(0, lo, part_acc[0, pl.ds(lo, rb_rows), :] + carry_in[rb])
        start_turn(0, rb)
        return carry

    lax.fori_loop(0, nrb, finish, 0)

    carry2_copy = pltpu.make_async_remote_copy(
        src_ref=carry2_out,
        dst_ref=carry2_in,
        send_sem=carry2_send,
        recv_sem=carry2_recv,
        device_id={"tm": lax.rem(tm + 1, ntm)},
        device_id_type=MESH,
    )
    inv2 = 1.0 / math.sqrt(nsubs_all)
    held = None
    for pair in range(last, -1, -1):

        def arrive(k, carry, pair=pair):
            turn_copy(pair, k, lax.rem(me + ndev - k, ndev)).wait_recv()
            return carry

        lax.fori_loop(1, ndev, arrive, 0)
        own_copy(pair).wait()
        merged = jnp.dot(recv_buf[pair], sel2[...], preferred_element_type=jnp.float32)
        if pair == last:
            carry2_out[...] = merged[:, 2 * ndm :]

            @pl.when(tm < ntm - 1)
            def _():
                carry2_copy.start()

        else:
            held = held + merged[:, 2 * ndm :]
            out_ref[2 * pair + 2] = held[:, :ndm] * inv2
            out_ref[2 * pair + 3] = held[:, ndm:] * inv2
        held = merged[:, : 2 * ndm]

    @pl.when(tm > 0)
    def _():
        carry2_copy.wait_recv()

    held = held + carry2_in[...]
    out_ref[0] = held[:, :ndm] * inv2
    out_ref[1] = held[:, ndm:] * inv2

    for k in range(1, ntm):
        stat_copy(k, tm).wait_send()

    @pl.when(tm < ntm - 1)
    def _():
        def sent(rb, carry):
            carry_copy(rb).wait_send()
            return carry

        lax.fori_loop(0, nrb, sent, 0)
        carry2_copy.wait_send()

    for pair in range(pairs):

        def left(k, carry, pair=pair):
            turn_copy(pair, k, me).wait_send()
            return carry

        lax.fori_loop(1, ndev, left, 0)


def body(voltages, rfi_mask, inner_delay, pick, outer_delay):
    rows, chans = voltages.shape[1], voltages.shape[3]
    ntm, nsub = lax.axis_size("tm"), lax.axis_size("sub")
    ndev = lax.axis_size("chan") * nsub
    ndm = pick.shape[1]
    ct = min(256, chans)
    ctiles = chans // ct
    pairs = rows // 2
    rb = 256
    nrb = BEAMS // rb
    lb = BEAMS // ndev
    cfg = dict(rows=rows, chans=chans, ct=ct, ntm=ntm, nsub=nsub, ndev=ndev, ndm=ndm, rb=rb)
    f32, bf16 = jnp.float32, jnp.bfloat16
    vm = pl.BlockSpec(memory_space=pltpu.VMEM)
    hbm = pl.BlockSpec(memory_space=pl.ANY)
    dma, steps = pltpu.SemaphoreType.DMA, rows * ctiles
    return pl.pallas_call(
        functools.partial(kernel, cfg),
        out_shape=jax.ShapeDtypeStruct((rows, lb, ndm), f32),
        in_specs=[hbm, vm, vm, hbm, vm, vm],
        out_specs=vm,
        scratch_shapes=[
            pltpu.VMEM((steps, 2, EW * NS, ct), bf16),
            pltpu.VMEM((rows, BEAMS, chans), bf16),
            pltpu.VMEM((EW, 2 * NS, ct), f32),
            pltpu.VMEM((EW, 2 * NS, ct), f32),
            pltpu.VMEM((NJ, chans), jnp.int32),
            pltpu.VMEM((2, 2 * LANES, chans), bf16),
            pltpu.VMEM((ndev * LANES, 4 * ndm), bf16),
            pltpu.VMEM((ctiles, 1, ct), f32),
            pltpu.VMEM((ctiles, 8, ct), f32),
            pltpu.VMEM((ctiles, 8, ct), f32),
            pltpu.VMEM((ntm, 2, chans), f32),
            pltpu.VMEM((pairs, BEAMS, LANES), f32),
            pltpu.VMEM((nrb, rb, LANES), f32),
            pltpu.VMEM((nrb, rb, LANES), f32),
            pltpu.VMEM((pairs, BEAMS, LANES), bf16),
            pltpu.VMEM((pairs, lb, ndev * LANES), bf16),
            pltpu.VMEM((lb, 2 * ndm), f32),
            pltpu.VMEM((lb, 2 * ndm), f32),
            dma((steps,)),
            dma,
            dma((ntm,)),
            dma((ntm,)),
            dma((nrb,)),
            dma((nrb,)),
            dma((pairs, ndev)),
            dma((pairs, ndev)),
            dma((pairs,)),
            dma,
            dma,
        ],
        compiler_params=pltpu.CompilerParams(
            collective_id=0, has_side_effects=True, vmem_limit_bytes=60 * 2**20
        ),
    )(
        voltages,
        jnp.asarray(dft_matrix(NS)),
        rfi_mask.reshape(1, chans),
        inner_delay.T,
        pick,
        outer_delay,
    )


def solution(mesh):
    placed = (
        P(None, ("groups", "tm"), None, ("chan", "sub")),
        P(("groups", "chan", "sub")),
        P(),
        P(),
        P(),
    )
    return jax.shard_map(
        body,
        mesh=mesh,
        in_specs=placed,
        out_specs=P(("groups", "tm"), ("chan", "sub"), None),
        check_vma=False,
    )
```

```python
import functools
import math

import jax
import jax.numpy as jnp
import numpy as np
from jax import lax
from jax.experimental import pallas as pl
from jax.experimental.pallas import tpu as pltpu
from jax.sharding import PartitionSpec as P

NS = 256
EW = 4
BEAMS = 1024
SUBW = 128
DIN = 2
DOUT = 2
NJ = 8
LANES = 128

eps_norm = 1e-05
MESH = pl.DeviceIdType.MESH


def dft_matrix(points):
    positions = np.arange(points, dtype=np.int32)
    products = positions[:, None] * positions[None, :] % points
    angle = products.astype(np.float32) * np.float32(2.0 * math.pi / points)
    half = points // 2
    cos, sin = np.cos(angle), np.sin(angle)
    table = np.concatenate([cos[:half], cos[half : half + 1], sin[1:half]], 0)
    return table.astype(jnp.bfloat16)


def kernel(
    cfg,
    volt_hbm,
    table_ref,
    mask_ref,
    delay_hbm,
    pick_ref,
    outer_ref,
    out_ref,
    vbuf,
    inten,
    field0,
    field1,
    delay_v,
    sel1,
    sel2,
    pilot,
    acc1,
    acc2,
    stats,
    part_acc,
    carry_out,
    carry_in,
    send_buf,
    recv_buf,
    carry2_out,
    carry2_in,
    vsem,
    dsem,
    stat_send,
    stat_recv,
    carry_send,
    carry_recv,
    turn_send,
    turn_recv,
    own_sem,
    carry2_send,
    carry2_recv,
):
    rows, chans, ct, ntm, nsub, ndev, ndm = (
        cfg["rows"], cfg["chans"], cfg["ct"], cfg["ntm"], cfg["nsub"], cfg["ndev"], cfg["ndm"],
    )
    pairs = rows // 2
    ctiles = chans // ct
    steps = rows * ctiles
    local_beams = BEAMS // ndev
    subs = chans // SUBW
    width = subs * NJ
    rb_rows = cfg["rb"]
    nrb = BEAMS // rb_rows
    tm = lax.axis_index("tm")
    me = lax.axis_index("chan") * nsub + lax.axis_index("sub")

    def peer_id(index):
        return {"chan": index // nsub, "sub": lax.rem(index, nsub)}

    def volt_copy(step):
        t, tile = step // ctiles, lax.rem(step, ctiles)
        return pltpu.make_async_copy(
            volt_hbm.at[:, t, :, pl.ds(pl.multiple_of(tile * ct, ct), ct)],
            vbuf.at[step],
            vsem.at[step],
        )

    def start_volt(step, carry):
        volt_copy(step).start()
        return carry

    lax.fori_loop(0, steps, start_volt, 0)
    delay_copy = pltpu.make_async_copy(
        delay_hbm.at[:, pl.ds(pl.multiple_of(me * chans, chans), chans)], delay_v, dsem
    )
    delay_copy.start()

    barrier = pltpu.get_barrier_semaphore()

    def greet_tm(k, carry):
        pl.semaphore_signal(
            barrier, inc=1, device_id={"tm": lax.rem(tm + k, ntm)}, device_id_type=MESH
        )
        return carry

    def greet_turn(k, carry):
        pl.semaphore_signal(
            barrier, inc=1, device_id=peer_id(lax.rem(me + k, ndev)), device_id_type=MESH
        )
        return carry

    lax.fori_loop(1, ntm, greet_tm, 0)
    lax.fori_loop(1, ndev, greet_turn, 0)

    pilot[...] = jnp.zeros_like(pilot)
    acc1[...] = jnp.zeros_like(acc1)
    acc2[...] = jnp.zeros_like(acc2)

    @pl.when(tm == 0)
    def _():
        carry_in[...] = jnp.zeros_like(carry_in)
        carry2_in[...] = jnp.zeros_like(carry2_in)

    def transform(step, field):
        volt_copy(step).wait()
        for e in range(EW):
            for part in range(2):
                block = vbuf[step, part, e * NS : (e + 1) * NS, :]
                field[e, part * NS : (part + 1) * NS, :] = jnp.dot(
                    table_ref[...], block, preferred_element_type=jnp.float32
                )

    CH, HALF = 8, NS // 2

    def detect(step, field):
        t, tile = step // ctiles, lax.rem(step, ctiles)
        col = pl.ds(pl.multiple_of(tile * ct, ct), ct)
        wide_row = pilot[tile]
        sums1, sums2 = [], []
        top = lax.broadcasted_iota(jnp.int32, (CH, LANES), 0) == 0
        for lane in range(0, ct, LANES):
            shift = jnp.broadcast_to(wide_row[:, lane : lane + LANES], (CH, LANES))
            s1 = jnp.zeros((8, LANES), jnp.float32)
            s2 = jnp.zeros((8, LANES), jnp.float32)
            here = pl.ds(pl.multiple_of(tile * ct + lane, LANES), LANES)
            for chunk in range(HALF // CH):
                lo = chunk * CH

                def part(index):
                    at = index * HALF + lo
                    return [field[e, at : at + CH, lane : lane + LANES] for e in range(EW)]

                ca, sb, cb, sa = part(0), part(1), part(2), part(3)
                if chunk == 0:
                    sa0 = [jnp.where(top, 0.0, v) for v in sa]
                    sb0 = [jnp.where(top, 0.0, v) for v in sb]
                else:
                    sa0, sb0 = sa, sb
                for mirror in range(2):
                    if mirror == 0:
                        re = [u + v for u, v in zip(ca, sa0)]
                        im = [u - v for u, v in zip(cb, sb0)]
                    else:
                        re = [u - v for u, v in zip(ca, sa0)]
                        im = [u + v for u, v in zip(cb, sb0)]
                        if chunk == 0:
                            re = [jnp.where(top, v, u) for u, v in zip(re, sb)]
                            im = [jnp.where(top, v, u) for u, v in zip(im, sa)]
                    ra, rb, rc, rd = re[0] + re[2], re[0] - re[2], re[1] + re[3], re[1] - re[3]
                    ia, ib, ic, id_ = im[0] + im[2], im[0] - im[2], im[1] + im[3], im[1] - im[3]
                    beam = [
                        (ra + rc, ia + ic),
                        (rb + id_, ib - rd),
                        (ra - rc, ia - ic),
                        (rb - id_, ib + rd),
                    ]
                    for q in range(EW):
                        x = beam[q][0] * beam[q][0] + beam[q][1] * beam[q][1]
                        x = x.astype(jnp.bfloat16)
                        at = q * NS + mirror * HALF + lo
                        inten[t, at : at + CH, here] = x
                        dev = x.astype(jnp.float32) - shift
                        s1 = s1 + dev
                        s2 = s2 + dev * dev
            sums1.append(s1)
            sums2.append(s2)
        s1, s2 = jnp.concatenate(sums1, 1), jnp.concatenate(sums2, 1)

        @pl.when(t > 0)
        def _():
            acc1[tile] += s1
            acc2[tile] += s2

        @pl.when(t == 0)
        def _():
            mean = jnp.sum(s1, axis=0, keepdims=True) * (1.0 / BEAMS)
            pilot[tile] = mean
            wide = jnp.broadcast_to(mean, (16, ct))

            def again(chunk, sums):
                r1, r2 = sums
                lo = pl.multiple_of(chunk * 64, 64)
                for i in range(4):
                    x = inten[0, pl.ds(lo + i * 16, 16), col].astype(jnp.float32)
                    dev = x - wide
                    sq = dev * dev
                    r1 = r1 + (dev[:8] + dev[8:])
                    r2 = r2 + (sq[:8] + sq[8:])
                return r1, r2

            zero = jnp.zeros((8, ct), jnp.float32)
            r1, r2 = lax.fori_loop(0, BEAMS // 64, again, (zero, zero))
            acc1[tile] = r1
            acc2[tile] = r2

    transform(0, field0)

    def two_steps(i, carry):
        transform(2 * i + 1, field1)
        detect(2 * i, field0)

        transform(2 * i + 2, field0)
        detect(2 * i + 1, field1)
        return carry

    lax.fori_loop(0, steps // 2 - 1, two_steps, 0)
    transform(steps - 1, field1)
    detect(steps - 2, field0)
    detect(steps - 1, field1)

    count = float(rows * BEAMS)
    for tile in range(ctiles):
        s1 = jnp.sum(acc1[tile], axis=0, keepdims=True)
        s2 = jnp.sum(acc2[tile], axis=0, keepdims=True)
        cols = slice(tile * ct, (tile + 1) * ct)
        stats[tm, 0:1, cols] = pilot[tile] + s1 * (1.0 / count)
        stats[tm, 1:2, cols] = s2 - s1 * s1 * (1.0 / count)

    pl.semaphore_wait(barrier, ntm - 1 + ndev - 1)

    def stat_copy(k, sender):
        return pltpu.make_async_remote_copy(
            src_ref=stats.at[tm],
            dst_ref=stats.at[sender],
            send_sem=stat_send.at[k],
            recv_sem=stat_recv.at[k],
            device_id={"tm": lax.rem(tm + k, ntm)},
            device_id_type=MESH,
        )

    for k in range(1, ntm):
        stat_copy(k, tm).start()
    delay_copy.wait()
    delays = delay_v[...].astype(jnp.float32)
    chan_sub = lax.broadcasted_iota(jnp.int32, (NJ, chans), 1) // SUBW
    for par_in in range(2):
        for half in range(2):
            pieces = []
            for group in range(LANES // NJ):
                par_out, sub = group // subs, group % subs
                lag = 2 * half + par_out - par_in
                if group < 2 * subs and 0 <= lag <= DIN:
                    hit = (delays == float(lag)) & (chan_sub == sub)
                    pieces.append(jnp.where(hit, 1.0, 0.0))
                else:
                    pieces.append(jnp.zeros((NJ, chans), jnp.float32))
            sel1[par_in, half * LANES : (half + 1) * LANES, :] = jnp.concatenate(
                pieces, 0
            ).astype(jnp.bfloat16)
    for k in range(1, ntm):
        stat_copy(k, lax.rem(tm + ntm - k, ntm)).wait_recv()
    means = [stats[i, 0:1, :] for i in range(ntm)]
    mean = sum(means[1:], means[0]) * (1.0 / ntm)
    spread = sum(stats[i, 1:2, :] for i in range(ntm))
    for i in range(ntm):
        spread = spread + count * ((means[i] - mean) * (means[i] - mean))
    var = spread * (1.0 / (count * ntm))
    scale = lax.rsqrt(var + eps_norm) * mask_ref[...].astype(jnp.float32)

    def carry_copy(rb):
        return pltpu.make_async_remote_copy(
            src_ref=carry_out.at[rb],
            dst_ref=carry_in.at[rb],
            send_sem=carry_send.at[rb],
            recv_sem=carry_recv.at[rb],
            device_id={"tm": lax.rem(tm + 1, ntm)},
            device_id_type=MESH,
        )

    def level1(pair, rb):
        lo = pl.multiple_of(rb * rb_rows, rb_rows)
        total = None
        for par in range(2):
            x = inten[2 * pair + par, pl.ds(lo, rb_rows), :].astype(jnp.float32)
            normed = ((x - mean) * scale).astype(jnp.bfloat16)
            term = lax.dot_general(
                normed, sel1[par], (((1,), (1,)), ((), ())), preferred_element_type=jnp.float32
            )
            total = term if total is None else total + term
        return lo, total

    inv1 = 1.0 / math.sqrt(SUBW)
    to_row = lax.broadcasted_iota(jnp.int32, (HALF, HALF), 0)
    from_row = lax.broadcasted_iota(jnp.int32, (HALF, HALF), 1)
    flip = jnp.where(lax.rem(to_row + from_row, HALF) == 0, 1.0, 0.0).astype(jnp.bfloat16)

    def put_send(pair, lo, total):
        ready = (total * inv1).astype(jnp.bfloat16)
        send_buf[pair, pl.ds(lo, HALF), :] = ready[:HALF]
        send_buf[pair, pl.ds(lo + HALF, HALF), :] = jnp.dot(
            flip, ready[HALF:], preferred_element_type=jnp.float32
        ).astype(jnp.bfloat16)

    def turn_copy(pair, k, sender):
        peer = lax.rem(me + k, ndev)
        return pltpu.make_async_remote_copy(
            src_ref=send_buf.at[
                pair, pl.ds(pl.multiple_of(peer * local_beams, local_beams), local_beams), :
            ],
            dst_ref=recv_buf.at[pair, :, pl.ds(pl.multiple_of(sender * LANES, LANES), LANES)],
            send_sem=turn_send.at[pair, k],
            recv_sem=turn_recv.at[pair, k],
            device_id=peer_id(peer),
            device_id_type=MESH,
        )

    def own_copy(pair):
        return pltpu.make_async_copy(
            send_buf.at[
                pair, pl.ds(pl.multiple_of(me * local_beams, local_beams), local_beams), :
            ],
            recv_buf.at[pair, :, pl.ds(pl.multiple_of(me * LANES, LANES), LANES)],
            own_sem.at[pair],
        )

    peers_rb = max(1, ndev // nrb)
    first_rb = me // peers_rb

    def start_turn(pair, rb):
        def one(i, carry):
            k = lax.rem(rb * peers_rb + i + ndev - me, ndev)

            @pl.when(k > 0)
            def _():
                turn_copy(pair, k, me).start()

            @pl.when(k == 0)
            def _():
                own_copy(pair).start()

            return carry

        lax.fori_loop(0, peers_rb, one, 0)

    last = pairs - 1
    def block(i, carry):
        rb = lax.rem(first_rb + i + 1, nrb)
        held = None
        for pair in range(last, -1, -1):
            lo, total = level1(pair, rb)
            if pair == last:
                carry_out[rb] = total[:, LANES:]
            else:
                put_send(pair + 1, lo, held + total[:, LANES:])
            held = total[:, :LANES]
        part_acc[rb] = held

        @pl.when(tm < ntm - 1)
        def _():
            carry_copy(rb).start()

        for pair in range(last, 0, -1):
            start_turn(pair, rb)
        return carry

    lax.fori_loop(0, nrb, block, 0)

    nsubs_all = subs * ndev
    code = (pick_ref[...] + NJ * outer_ref[...]).astype(jnp.float32).astype(jnp.bfloat16)

    def make_sel2(dev, carry):
        q = lax.broadcasted_iota(jnp.int32, (LANES, nsubs_all), 0)
        which = dev * subs + lax.rem(q, width) // NJ
        expand = jnp.where(
            which == lax.broadcasted_iota(jnp.int32, (LANES, nsubs_all), 1), 1.0, 0.0
        ).astype(jnp.bfloat16)
        spread = jnp.dot(expand, code, preferred_element_type=jnp.float32)
        q = lax.broadcasted_iota(jnp.int32, (LANES, ndm), 0)
        slot = lax.rem(q, NJ)
        par_in = q // width
        base = pl.multiple_of(dev * LANES, LANES)
        for half in range(2):
            for par_out in range(2):
                lag = 2 * half + par_out - par_in
                want = (slot + NJ * lag).astype(jnp.float32)
                hit = (spread == want) & (lag >= 0) & (lag <= DOUT) & (par_in < 2)
                col = (2 * half + par_out) * ndm
                sel2[pl.ds(base, LANES), col : col + ndm] = jnp.where(hit, 1.0, 0.0).astype(
                    jnp.bfloat16
                )
        return carry

    lax.fori_loop(0, ndev, make_sel2, 0)

    def finish(i, carry):
        rb = lax.rem(first_rb + i + 1, nrb)

        @pl.when(tm > 0)
        def _():
            carry_copy(rb).wait_recv()

        lo = pl.multiple_of(rb * rb_rows, rb_rows)
        put_send(0, lo, part_acc[rb] + carry_in[rb])
        start_turn(0, rb)
        return carry

    lax.fori_loop(0, nrb, finish, 0)

    carry2_copy = pltpu.make_async_remote_copy(
        src_ref=carry2_out,
        dst_ref=carry2_in,
        send_sem=carry2_send,
        recv_sem=carry2_recv,
        device_id={"tm": lax.rem(tm + 1, ntm)},
        device_id_type=MESH,
    )
    inv2 = 1.0 / math.sqrt(nsubs_all)
    held = None
    for pair in range(last, -1, -1):

        def arrive(k, carry, pair=pair):
            turn_copy(pair, k, lax.rem(me + ndev - k, ndev)).wait_recv()
            return carry

        lax.fori_loop(1, ndev, arrive, 0)
        own_copy(pair).wait()
        merged = jnp.dot(recv_buf[pair], sel2[...], preferred_element_type=jnp.float32)
        if pair == last:
            carry2_out[...] = merged[:, 2 * ndm :]

            @pl.when(tm < ntm - 1)
            def _():
                carry2_copy.start()

        else:
            held = held + merged[:, 2 * ndm :]
            out_ref[2 * pair + 2] = held[:, :ndm] * inv2
            out_ref[2 * pair + 3] = held[:, ndm:] * inv2
        held = merged[:, : 2 * ndm]

    @pl.when(tm > 0)
    def _():
        carry2_copy.wait_recv()

    held = held + carry2_in[...]
    out_ref[0] = held[:, :ndm] * inv2
    out_ref[1] = held[:, ndm:] * inv2

    for k in range(1, ntm):
        stat_copy(k, tm).wait_send()

    @pl.when(tm < ntm - 1)
    def _():
        def sent(rb, carry):
            carry_copy(rb).wait_send()
            return carry

        lax.fori_loop(0, nrb, sent, 0)
        carry2_copy.wait_send()

    for pair in range(pairs):

        def left(k, carry, pair=pair):
            turn_copy(pair, k, me).wait_send()
            return carry

        lax.fori_loop(1, ndev, left, 0)


def body(voltages, rfi_mask, inner_delay, pick, outer_delay):
    rows, chans = voltages.shape[1], voltages.shape[3]
    ntm, nsub = lax.axis_size("tm"), lax.axis_size("sub")
    ndev = lax.axis_size("chan") * nsub
    ndm = pick.shape[1]
    ct = min(256, chans)
    ctiles = chans // ct
    pairs = rows // 2
    rb = 256
    nrb = BEAMS // rb
    lb = BEAMS // ndev
    cfg = dict(rows=rows, chans=chans, ct=ct, ntm=ntm, nsub=nsub, ndev=ndev, ndm=ndm, rb=rb)
    f32, bf16 = jnp.float32, jnp.bfloat16
    vm = pl.BlockSpec(memory_space=pltpu.VMEM)
    hbm = pl.BlockSpec(memory_space=pl.ANY)
    dma, steps = pltpu.SemaphoreType.DMA, rows * ctiles
    return pl.pallas_call(
        functools.partial(kernel, cfg),
        out_shape=jax.ShapeDtypeStruct((rows, lb, ndm), f32),
        in_specs=[hbm, vm, vm, hbm, vm, vm],
        out_specs=vm,
        scratch_shapes=[
            pltpu.VMEM((steps, 2, EW * NS, ct), bf16),
            pltpu.VMEM((rows, BEAMS, chans), bf16),
            pltpu.VMEM((EW, 2 * NS, ct), f32),
            pltpu.VMEM((EW, 2 * NS, ct), f32),
            pltpu.VMEM((NJ, chans), jnp.int32),
            pltpu.VMEM((2, 2 * LANES, chans), bf16),
            pltpu.VMEM((ndev * LANES, 4 * ndm), bf16),
            pltpu.VMEM((ctiles, 1, ct), f32),
            pltpu.VMEM((ctiles, 8, ct), f32),
            pltpu.VMEM((ctiles, 8, ct), f32),
            pltpu.VMEM((ntm, 2, chans), f32),
            pltpu.VMEM((nrb, rb, LANES), f32),
            pltpu.VMEM((nrb, rb, LANES), f32),
            pltpu.VMEM((nrb, rb, LANES), f32),
            pltpu.VMEM((pairs, BEAMS, LANES), bf16),
            pltpu.VMEM((pairs, lb, ndev * LANES), bf16),
            pltpu.VMEM((lb, 2 * ndm), f32),
            pltpu.VMEM((lb, 2 * ndm), f32),
            dma((steps,)),
            dma,
            dma((ntm,)),
            dma((ntm,)),
            dma((nrb,)),
            dma((nrb,)),
            dma((pairs, ndev)),
            dma((pairs, ndev)),
            dma((pairs,)),
            dma,
            dma,
        ],
        compiler_params=pltpu.CompilerParams(
            collective_id=0, has_side_effects=True, vmem_limit_bytes=60 * 2**20
        ),
    )(
        voltages,
        jnp.asarray(dft_matrix(NS)),
        rfi_mask.reshape(1, chans),
        inner_delay.T,
        pick,
        outer_delay,
    )


def solution(mesh):
    placed = (
        P(None, ("groups", "tm"), None, ("chan", "sub")),
        P(("groups", "chan", "sub")),
        P(),
        P(),
        P(),
    )
    return jax.shard_map(
        body,
        mesh=mesh,
        in_specs=placed,
        out_specs=P(("groups", "tm"), ("chan", "sub"), None),
        check_vma=False,
    )
```

```python
import functools
import math

import jax
import jax.numpy as jnp
import numpy as np
from jax import lax
from jax.experimental import pallas as pl
from jax.experimental.pallas import tpu as pltpu
from jax.sharding import PartitionSpec as P

NS = 256
EW = 4
BEAMS = 1024
SUBW = 128
DIN = 2
DOUT = 2
NJ = 8
LANES = 128

eps_norm = 1e-05
MESH = pl.DeviceIdType.MESH


def dft_matrix(points):
    positions = np.arange(points, dtype=np.int32)
    products = positions[:, None] * positions[None, :] % points
    angle = products.astype(np.float32) * np.float32(2.0 * math.pi / points)
    half = points // 2
    cos, sin = np.cos(angle), np.sin(angle)
    table = np.concatenate([cos[:half], cos[half : half + 1], sin[1:half]], 0)
    return table.astype(jnp.bfloat16)


def kernel(
    cfg,
    volt_hbm,
    table_hbm,
    mask_hbm,
    delay_hbm,
    pick_hbm,
    outer_hbm,
    out_ref,
    table_ref,
    mask_ref,
    pick_ref,
    outer_ref,
    vbuf,
    inten,
    field0,
    field1,
    delay_v,
    sel1,
    sel2,
    pilot,
    acc1,
    acc2,
    stats,
    part_acc,
    carry_out,
    carry_in,
    send_buf,
    recv_buf,
    carry2_out,
    carry2_in,
    small_sem,
    vsem,
    dsem,
    stat_send,
    stat_recv,
    carry_send,
    carry_recv,
    turn_send,
    turn_recv,
    own_sem,
    carry2_send,
    carry2_recv,
):
    rows, chans, ct, ntm, nsub, ndev, ndm = (
        cfg["rows"], cfg["chans"], cfg["ct"], cfg["ntm"], cfg["nsub"], cfg["ndev"], cfg["ndm"],
    )
    pairs = rows // 2
    ctiles = chans // ct
    steps = rows * ctiles
    local_beams = BEAMS // ndev
    subs = chans // SUBW
    width = subs * NJ
    rb_rows = cfg["rb"]
    nrb = BEAMS // rb_rows
    tm = lax.axis_index("tm")
    me = lax.axis_index("chan") * nsub + lax.axis_index("sub")

    def peer_id(index):
        return {"chan": index // nsub, "sub": lax.rem(index, nsub)}

    def volt_copy(step):
        t, tile = step // ctiles, lax.rem(step, ctiles)
        return pltpu.make_async_copy(
            volt_hbm.at[:, t, :, pl.ds(pl.multiple_of(tile * ct, ct), ct)],
            vbuf.at[step],
            vsem.at[step],
        )

    table_copy = pltpu.make_async_copy(table_hbm, table_ref, small_sem.at[0])
    mask_copy = pltpu.make_async_copy(mask_hbm, mask_ref, small_sem.at[1])
    pick_copy = pltpu.make_async_copy(pick_hbm, pick_ref, small_sem.at[2])
    outer_copy = pltpu.make_async_copy(outer_hbm, outer_ref, small_sem.at[3])
    table_copy.start()

    def start_volt(step, carry):
        volt_copy(step).start()
        return carry

    lax.fori_loop(0, steps, start_volt, 0)
    delay_copy = pltpu.make_async_copy(
        delay_hbm.at[:, pl.ds(pl.multiple_of(me * chans, chans), chans)], delay_v, dsem
    )
    delay_copy.start()
    mask_copy.start()
    pick_copy.start()
    outer_copy.start()

    barrier = pltpu.get_barrier_semaphore()

    def greet_tm(k, carry):
        pl.semaphore_signal(
            barrier, inc=1, device_id={"tm": lax.rem(tm + k, ntm)}, device_id_type=MESH
        )
        return carry

    def greet_turn(k, carry):
        pl.semaphore_signal(
            barrier, inc=1, device_id=peer_id(lax.rem(me + k, ndev)), device_id_type=MESH
        )
        return carry

    lax.fori_loop(1, ntm, greet_tm, 0)
    lax.fori_loop(1, ndev, greet_turn, 0)

    pilot[...] = jnp.zeros_like(pilot)
    acc1[...] = jnp.zeros_like(acc1)
    acc2[...] = jnp.zeros_like(acc2)

    @pl.when(tm == 0)
    def _():
        carry_in[...] = jnp.zeros_like(carry_in)
        carry2_in[...] = jnp.zeros_like(carry2_in)

    def transform(step, field):
        volt_copy(step).wait()
        for e in range(EW):
            for part in range(2):
                block = vbuf[step, part, e * NS : (e + 1) * NS, :]
                field[e, part * NS : (part + 1) * NS, :] = jnp.dot(
                    table_ref[...], block, preferred_element_type=jnp.float32
                )

    CH, HALF = 8, NS // 2

    def detect(step, field):
        t, tile = step // ctiles, lax.rem(step, ctiles)
        col = pl.ds(pl.multiple_of(tile * ct, ct), ct)
        wide_row = pilot[tile]
        sums1, sums2 = [], []
        top = lax.broadcasted_iota(jnp.int32, (CH, LANES), 0) == 0
        for lane in range(0, ct, LANES):
            shift = jnp.broadcast_to(wide_row[:, lane : lane + LANES], (CH, LANES))
            s1 = jnp.zeros((8, LANES), jnp.float32)
            s2 = jnp.zeros((8, LANES), jnp.float32)
            here = pl.ds(pl.multiple_of(tile * ct + lane, LANES), LANES)
            for chunk in range(HALF // CH):
                lo = chunk * CH

                def part(index):
                    at = index * HALF + lo
                    return [field[e, at : at + CH, lane : lane + LANES] for e in range(EW)]

                ca, sb, cb, sa = part(0), part(1), part(2), part(3)
                if chunk == 0:
                    sa0 = [jnp.where(top, 0.0, v) for v in sa]
                    sb0 = [jnp.where(top, 0.0, v) for v in sb]
                else:
                    sa0, sb0 = sa, sb
                for mirror in range(2):
                    if mirror == 0:
                        re = [u + v for u, v in zip(ca, sa0)]
                        im = [u - v for u, v in zip(cb, sb0)]
                    else:
                        re = [u - v for u, v in zip(ca, sa0)]
                        im = [u + v for u, v in zip(cb, sb0)]
                        if chunk == 0:
                            re = [jnp.where(top, v, u) for u, v in zip(re, sb)]
                            im = [jnp.where(top, v, u) for u, v in zip(im, sa)]
                    ra, rb, rc, rd = re[0] + re[2], re[0] - re[2], re[1] + re[3], re[1] - re[3]
                    ia, ib, ic, id_ = im[0] + im[2], im[0] - im[2], im[1] + im[3], im[1] - im[3]
                    beam = [
                        (ra + rc, ia + ic),
                        (rb + id_, ib - rd),
                        (ra - rc, ia - ic),
                        (rb - id_, ib + rd),
                    ]
                    for q in range(EW):
                        x = beam[q][0] * beam[q][0] + beam[q][1] * beam[q][1]
                        x = x.astype(jnp.bfloat16)
                        at = q * NS + mirror * HALF + lo
                        inten[t, at : at + CH, here] = x
                        dev = x.astype(jnp.float32) - shift
                        s1 = s1 + dev
                        s2 = s2 + dev * dev
            sums1.append(s1)
            sums2.append(s2)
        s1, s2 = jnp.concatenate(sums1, 1), jnp.concatenate(sums2, 1)

        @pl.when(t > 0)
        def _():
            acc1[tile] += s1
            acc2[tile] += s2

        @pl.when(t == 0)
        def _():
            mean = jnp.sum(s1, axis=0, keepdims=True) * (1.0 / BEAMS)
            pilot[tile] = mean
            wide = jnp.broadcast_to(mean, (16, ct))

            def again(chunk, sums):
                r1, r2 = sums
                lo = pl.multiple_of(chunk * 64, 64)
                for i in range(4):
                    x = inten[0, pl.ds(lo + i * 16, 16), col].astype(jnp.float32)
                    dev = x - wide
                    sq = dev * dev
                    r1 = r1 + (dev[:8] + dev[8:])
                    r2 = r2 + (sq[:8] + sq[8:])
                return r1, r2

            zero = jnp.zeros((8, ct), jnp.float32)
            r1, r2 = lax.fori_loop(0, BEAMS // 64, again, (zero, zero))
            acc1[tile] = r1
            acc2[tile] = r2

    table_copy.wait()
    transform(0, field0)

    def two_steps(i, carry):
        transform(2 * i + 1, field1)
        detect(2 * i, field0)

        transform(2 * i + 2, field0)
        detect(2 * i + 1, field1)
        return carry

    lax.fori_loop(0, steps // 2 - 1, two_steps, 0)
    transform(steps - 1, field1)
    detect(steps - 2, field0)
    detect(steps - 1, field1)

    count = float(rows * BEAMS)
    for tile in range(ctiles):
        s1 = jnp.sum(acc1[tile], axis=0, keepdims=True)
        s2 = jnp.sum(acc2[tile], axis=0, keepdims=True)
        cols = slice(tile * ct, (tile + 1) * ct)
        stats[tm, 0:1, cols] = pilot[tile] + s1 * (1.0 / count)
        stats[tm, 1:2, cols] = s2 - s1 * s1 * (1.0 / count)

    pl.semaphore_wait(barrier, ntm - 1 + ndev - 1)

    def stat_copy(k, sender):
        return pltpu.make_async_remote_copy(
            src_ref=stats.at[tm],
            dst_ref=stats.at[sender],
            send_sem=stat_send.at[k],
            recv_sem=stat_recv.at[k],
            device_id={"tm": lax.rem(tm + k, ntm)},
            device_id_type=MESH,
        )

    for k in range(1, ntm):
        stat_copy(k, tm).start()
    delay_copy.wait()
    mask_copy.wait()
    pick_copy.wait()
    outer_copy.wait()
    delays = delay_v[...].astype(jnp.float32)
    chan_sub = lax.broadcasted_iota(jnp.int32, (NJ, chans), 1) // SUBW
    for par_in in range(2):
        for half in range(2):
            pieces = []
            for group in range(LANES // NJ):
                par_out, sub = group // subs, group % subs
                lag = 2 * half + par_out - par_in
                if group < 2 * subs and 0 <= lag <= DIN:
                    hit = (delays == float(lag)) & (chan_sub == sub)
                    pieces.append(jnp.where(hit, 1.0, 0.0))
                else:
                    pieces.append(jnp.zeros((NJ, chans), jnp.float32))
            sel1[par_in, half * LANES : (half + 1) * LANES, :] = jnp.concatenate(
                pieces, 0
            ).astype(jnp.bfloat16)
    for k in range(1, ntm):
        stat_copy(k, lax.rem(tm + ntm - k, ntm)).wait_recv()
    means = [stats[i, 0:1, :] for i in range(ntm)]
    mean = sum(means[1:], means[0]) * (1.0 / ntm)
    spread = sum(stats[i, 1:2, :] for i in range(ntm))
    for i in range(ntm):
        spread = spread + count * ((means[i] - mean) * (means[i] - mean))
    var = spread * (1.0 / (count * ntm))
    scale = lax.rsqrt(var + eps_norm) * mask_ref[...].astype(jnp.float32)

    def carry_copy(rb):
        return pltpu.make_async_remote_copy(
            src_ref=carry_out.at[rb],
            dst_ref=carry_in.at[rb],
            send_sem=carry_send.at[rb],
            recv_sem=carry_recv.at[rb],
            device_id={"tm": lax.rem(tm + 1, ntm)},
            device_id_type=MESH,
        )

    def level1(pair, rb):
        lo = pl.multiple_of(rb * rb_rows, rb_rows)
        total = None
        for par in range(2):
            x = inten[2 * pair + par, pl.ds(lo, rb_rows), :].astype(jnp.float32)
            normed = ((x - mean) * scale).astype(jnp.bfloat16)
            term = lax.dot_general(
                normed, sel1[par], (((1,), (1,)), ((), ())), preferred_element_type=jnp.float32
            )
            total = term if total is None else total + term
        return lo, total

    inv1 = 1.0 / math.sqrt(SUBW)
    to_row = lax.broadcasted_iota(jnp.int32, (HALF, HALF), 0)
    from_row = lax.broadcasted_iota(jnp.int32, (HALF, HALF), 1)
    flip = jnp.where(lax.rem(to_row + from_row, HALF) == 0, 1.0, 0.0).astype(jnp.bfloat16)

    def put_send(pair, lo, total):
        ready = (total * inv1).astype(jnp.bfloat16)
        send_buf[pair, pl.ds(lo, HALF), :] = ready[:HALF]
        send_buf[pair, pl.ds(lo + HALF, HALF), :] = jnp.dot(
            flip, ready[HALF:], preferred_element_type=jnp.float32
        ).astype(jnp.bfloat16)

    def turn_copy(pair, k, sender):
        peer = lax.rem(me + k, ndev)
        return pltpu.make_async_remote_copy(
            src_ref=send_buf.at[
                pair, pl.ds(pl.multiple_of(peer * local_beams, local_beams), local_beams), :
            ],
            dst_ref=recv_buf.at[pair, :, pl.ds(pl.multiple_of(sender * LANES, LANES), LANES)],
            send_sem=turn_send.at[pair, k],
            recv_sem=turn_recv.at[pair, k],
            device_id=peer_id(peer),
            device_id_type=MESH,
        )

    def own_copy(pair):
        return pltpu.make_async_copy(
            send_buf.at[
                pair, pl.ds(pl.multiple_of(me * local_beams, local_beams), local_beams), :
            ],
            recv_buf.at[pair, :, pl.ds(pl.multiple_of(me * LANES, LANES), LANES)],
            own_sem.at[pair],
        )

    peers_rb = max(1, ndev // nrb)
    first_rb = me // peers_rb

    def start_turn(pair, rb):
        def one(i, carry):
            k = lax.rem(rb * peers_rb + i + ndev - me, ndev)

            @pl.when(k > 0)
            def _():
                turn_copy(pair, k, me).start()

            @pl.when(k == 0)
            def _():
                own_copy(pair).start()

            return carry

        lax.fori_loop(0, peers_rb, one, 0)

    last = pairs - 1
    def block(i, carry):
        rb = lax.rem(first_rb + i + 1, nrb)
        held = None
        for pair in range(last, -1, -1):
            lo, total = level1(pair, rb)
            if pair == last:
                carry_out[rb] = total[:, LANES:]
            else:
                put_send(pair + 1, lo, held + total[:, LANES:])
            held = total[:, :LANES]
        part_acc[rb] = held

        @pl.when(tm < ntm - 1)
        def _():
            carry_copy(rb).start()

        for pair in range(last, 0, -1):
            start_turn(pair, rb)
        return carry

    lax.fori_loop(0, nrb, block, 0)

    nsubs_all = subs * ndev
    code = (pick_ref[...] + NJ * outer_ref[...]).astype(jnp.float32).astype(jnp.bfloat16)

    def make_sel2(dev, carry):
        q = lax.broadcasted_iota(jnp.int32, (LANES, nsubs_all), 0)
        which = dev * subs + lax.rem(q, width) // NJ
        expand = jnp.where(
            which == lax.broadcasted_iota(jnp.int32, (LANES, nsubs_all), 1), 1.0, 0.0
        ).astype(jnp.bfloat16)
        spread = jnp.dot(expand, code, preferred_element_type=jnp.float32)
        q = lax.broadcasted_iota(jnp.int32, (LANES, ndm), 0)
        slot = lax.rem(q, NJ)
        par_in = q // width
        base = pl.multiple_of(dev * LANES, LANES)
        for half in range(2):
            for par_out in range(2):
                lag = 2 * half + par_out - par_in
                want = (slot + NJ * lag).astype(jnp.float32)
                hit = (spread == want) & (lag >= 0) & (lag <= DOUT) & (par_in < 2)
                col = (2 * half + par_out) * ndm
                sel2[pl.ds(base, LANES), col : col + ndm] = jnp.where(hit, 1.0, 0.0).astype(
                    jnp.bfloat16
                )
        return carry

    lax.fori_loop(0, ndev, make_sel2, 0)

    def finish(i, carry):
        rb = lax.rem(first_rb + i + 1, nrb)

        @pl.when(tm > 0)
        def _():
            carry_copy(rb).wait_recv()

        lo = pl.multiple_of(rb * rb_rows, rb_rows)
        put_send(0, lo, part_acc[rb] + carry_in[rb])
        start_turn(0, rb)
        return carry

    lax.fori_loop(0, nrb, finish, 0)

    carry2_copy = pltpu.make_async_remote_copy(
        src_ref=carry2_out,
        dst_ref=carry2_in,
        send_sem=carry2_send,
        recv_sem=carry2_recv,
        device_id={"tm": lax.rem(tm + 1, ntm)},
        device_id_type=MESH,
    )
    inv2 = 1.0 / math.sqrt(nsubs_all)
    held = None
    for pair in range(last, -1, -1):

        def arrive(k, carry, pair=pair):
            turn_copy(pair, k, lax.rem(me + ndev - k, ndev)).wait_recv()
            return carry

        lax.fori_loop(1, ndev, arrive, 0)
        own_copy(pair).wait()
        merged = jnp.dot(recv_buf[pair], sel2[...], preferred_element_type=jnp.float32)
        if pair == last:
            carry2_out[...] = merged[:, 2 * ndm :]

            @pl.when(tm < ntm - 1)
            def _():
                carry2_copy.start()

        else:
            held = held + merged[:, 2 * ndm :]
            out_ref[2 * pair + 2] = held[:, :ndm] * inv2
            out_ref[2 * pair + 3] = held[:, ndm:] * inv2
        held = merged[:, : 2 * ndm]

    @pl.when(tm > 0)
    def _():
        carry2_copy.wait_recv()

    held = held + carry2_in[...]
    out_ref[0] = held[:, :ndm] * inv2
    out_ref[1] = held[:, ndm:] * inv2

    for k in range(1, ntm):
        stat_copy(k, tm).wait_send()

    @pl.when(tm < ntm - 1)
    def _():
        def sent(rb, carry):
            carry_copy(rb).wait_send()
            return carry

        lax.fori_loop(0, nrb, sent, 0)
        carry2_copy.wait_send()

    for pair in range(pairs):

        def left(k, carry, pair=pair):
            turn_copy(pair, k, me).wait_send()
            return carry

        lax.fori_loop(1, ndev, left, 0)


def body(voltages, rfi_mask, inner_delay, pick, outer_delay):
    rows, chans = voltages.shape[1], voltages.shape[3]
    ntm, nsub = lax.axis_size("tm"), lax.axis_size("sub")
    ndev = lax.axis_size("chan") * nsub
    ndm = pick.shape[1]
    ct = min(256, chans)
    ctiles = chans // ct
    pairs = rows // 2
    rb = 256
    nrb = BEAMS // rb
    lb = BEAMS // ndev
    cfg = dict(rows=rows, chans=chans, ct=ct, ntm=ntm, nsub=nsub, ndev=ndev, ndm=ndm, rb=rb)
    f32, bf16 = jnp.float32, jnp.bfloat16
    vm = pl.BlockSpec(memory_space=pltpu.VMEM)
    hbm = pl.BlockSpec(memory_space=pl.ANY)
    dma, steps = pltpu.SemaphoreType.DMA, rows * ctiles
    return pl.pallas_call(
        functools.partial(kernel, cfg),
        out_shape=jax.ShapeDtypeStruct((rows, lb, ndm), f32),
        in_specs=[hbm] * 6,
        out_specs=vm,
        scratch_shapes=[
            pltpu.VMEM((NS, NS), bf16),
            pltpu.VMEM((1, chans), jnp.int32),
            pltpu.VMEM(pick.shape, jnp.int32),
            pltpu.VMEM(outer_delay.shape, jnp.int32),
            pltpu.VMEM((steps, 2, EW * NS, ct), bf16),
            pltpu.VMEM((rows, BEAMS, chans), bf16),
            pltpu.VMEM((EW, 2 * NS, ct), f32),
            pltpu.VMEM((EW, 2 * NS, ct), f32),
            pltpu.VMEM((NJ, chans), jnp.int32),
            pltpu.VMEM((2, 2 * LANES, chans), bf16),
            pltpu.VMEM((ndev * LANES, 4 * ndm), bf16),
            pltpu.VMEM((ctiles, 1, ct), f32),
            pltpu.VMEM((ctiles, 8, ct), f32),
            pltpu.VMEM((ctiles, 8, ct), f32),
            pltpu.VMEM((ntm, 2, chans), f32),
            pltpu.VMEM((nrb, rb, LANES), f32),
            pltpu.VMEM((nrb, rb, LANES), f32),
            pltpu.VMEM((nrb, rb, LANES), f32),
            pltpu.VMEM((pairs, BEAMS, LANES), bf16),
            pltpu.VMEM((pairs, lb, ndev * LANES), bf16),
            pltpu.VMEM((lb, 2 * ndm), f32),
            pltpu.VMEM((lb, 2 * ndm), f32),
            dma((4,)),
            dma((steps,)),
            dma,
            dma((ntm,)),
            dma((ntm,)),
            dma((nrb,)),
            dma((nrb,)),
            dma((pairs, ndev)),
            dma((pairs, ndev)),
            dma((pairs,)),
            dma,
            dma,
        ],
        compiler_params=pltpu.CompilerParams(
            collective_id=0, has_side_effects=True, vmem_limit_bytes=60 * 2**20
        ),
    )(
        voltages,
        jnp.asarray(dft_matrix(NS)),
        rfi_mask.reshape(1, chans),
        inner_delay.T,
        pick,
        outer_delay,
    )


def solution(mesh):
    placed = (
        P(None, ("groups", "tm"), None, ("chan", "sub")),
        P(("groups", "chan", "sub")),
        P(),
        P(),
        P(),
    )
    return jax.shard_map(
        body,
        mesh=mesh,
        in_specs=placed,
        out_specs=P(("groups", "tm"), ("chan", "sub"), None),
        check_vma=False,
    )
```
